32 devices in a mesh: layer: 8 (over z, x), lat: 4 (over y, core).
Axes of the slice: x: 2, y: 2, z: 4, core: 2. Of those that a mesh axis runs over, the one named last changes fastest.
Arguments:
- inverse: bfloat16 [8, 8, 512, 512], P('layer', 'lat')
- tiles: bfloat16 [1024, 256], P(('layer', 'lat')), may hold values from -6 to 6
- tile_dest: int32 [1024, 1], P(('layer', 'lat')), may hold values from 0 to 31; in each aligned block of 32 rows (0 to 31, 32 to 63, ...) at most 2 rows name the same one
- tile_code: int32 [1024], P(('layer', 'lat')), may hold values from 0 to 31
Outputs:
- solution: float32 [8, 8, 8, 512], P('layer', 'lat')
The draws below stay inside these ranges and needn't reach their ends.
Inputs may be any that keep to these rules, and one draw needn't show every extreme that they name: `tile_dest`: the rows of one device name any one device at most 2 times; in every draw some device's rows name some device exactly 2 times.
All inputs are finite; a program needn't handle non-finite values.
Results may differ from the reference program's by a relative error of at most 0.004.
Values may be sent and summed in bfloat16 or wider, within the bound.
A program may use at most 128 MiB of HBM per device.

```python
import math
import jax
import jax.numpy as jnp
import numpy as np
from jax import lax

BLOCK = 128
DEP = 2
SRC = 8
NB = 2
CAP = 2
M = 512
BLOCKS = 8
TPD = 32
TILES = 1024
N_LAYER = 8
N_LAT = 4


def draw_inverse(key, part):
    entire_extent = (N_LAYER, NB * N_LAT, M, M)
    trace_len = 2 * BLOCK
    far_rows = trace_len * (DEP - 1)
    perturbation_seed, principal_seed, damping_seed, spike_seed, surviving_seed = jax.random.split(key, 5)
    row_at = lax.broadcasted_iota(jnp.int32, entire_extent, 2)
    col_at = lax.broadcasted_iota(jnp.int32, entire_extent, 3)
    noise = jax.random.normal(perturbation_seed, entire_extent, jnp.float32) * (0.3 / math.sqrt(M))
    diagonal = jax.random.uniform(principal_seed, entire_extent, jnp.float32, 0.8, 1.6)
    low_rate = 0.5 / N_LAYER
    high_rate = 2.0
    damping_multiplier = jnp.exp(jax.random.uniform(damping_seed, entire_extent, jnp.float32, math.log(low_rate), math.log(high_rate)))
    spike_occurrences = jax.random.uniform(spike_seed, entire_extent, jnp.float32) < 3.0 / N_LAYER
    surviving_proportion = jax.random.uniform(surviving_seed, entire_extent, jnp.float32, 0.5, 0.8)
    leftover_amount = jnp.exp(-damping_multiplier) * jnp.where(spike_occurrences, surviving_proportion, 1.0)
    lower_band = (row_at >= far_rows) & (col_at == row_at - far_rows)
    upper_band = (row_at < trace_len) & (col_at == row_at + far_rows)
    entries = noise + jnp.where(row_at == col_at, diagonal, 0.0) + jnp.where(lower_band | upper_band, leftover_amount, 0.0)
    return entries.astype(jnp.bfloat16)


def touch_ends(values, own_key, smallest, high):
    spot = [jax.random.randint(jax.random.fold_in(own_key, axis), (), 0, length) for axis, length in enumerate(values.shape)]
    longest = values.shape.index(max(values.shape))
    next_to = spot[:longest] + [(spot[longest] + 1) % values.shape[longest]] + spot[longest + 1:]
    return values.at[tuple(spot)].set(smallest).at[tuple(next_to)].set(high)


def block_levels(rng, shape, cuts, low, high):
    gain, own = 1.0, jax.random.fold_in(rng, 6)
    for position, shards_of in cuts:
        heights = jnp.exp(jax.random.uniform(jax.random.fold_in(own, position), (shards_of,), jnp.float32, low / len(cuts), high / len(cuts)))
        gain = gain * jnp.repeat(heights, shape[position] // shards_of).reshape([-1 if axis == position else 1 for axis in range(len(shape))])
    return gain


def assign_block(stream_key, own, number, rows, amount, top, reach, slope):
    order = jax.random.permutation(stream_key, amount)
    heavy_load, usual = shares(amount, rows * top, reach, slope, True), shares(amount, rows * top, reach, slope, False)
    places = jnp.arange(amount)

    def named(tallies, rotation):
        used = int((tallies > 0).sum())
        fixed = max(1, used // 4)
        shifted = fixed + (places - fixed + rotation * (used - fixed)) % max(1, amount - fixed)
        return jnp.zeros((amount,), jnp.int32).at[order[jnp.where(places < fixed, places, shifted)]].set(jnp.asarray(tallies, jnp.int32))

    tallies = jnp.where(number % 4 == 0, named(heavy_load, number // 4), named(usual, number - number // 4 - 1))
    mixed = jax.random.permutation(jax.random.fold_in(own, 3), amount)
    source_of, sink = mixed[0:amount // 2 * 2:2], mixed[1:amount // 2 * 2:2]
    slack = jnp.minimum(tallies[source_of] - 1, reach - tallies[sink]) // 2
    slack = jnp.where((source_of == order[0]) | (sink == order[0]) | (tallies[sink] == 0), 0, jnp.maximum(slack, 0))
    shifted = jax.random.randint(jax.random.fold_in(own, 4), (amount // 2,), 0, 1 << 20) % (slack + 1)
    tallies = tallies.at[source_of].add(-shifted).at[sink].add(shifted)
    items = jnp.searchsorted(jnp.cumsum(tallies), jnp.arange(rows * top), side="right").astype(jnp.int32)
    grid = items.reshape(top, rows).T
    grid = grid[jax.random.permutation(jax.random.fold_in(own, 1), rows)]
    rotation = jax.random.randint(jax.random.fold_in(own, 2), (rows, 1), 0, top)
    return jnp.take_along_axis(grid, (jnp.arange(top)[None, :] + rotation) % top, axis=1)


def shares(amount, total, bound, slope, full):
    portions = [(1 << 20) // math.isqrt(standing ** slope) + 1 for standing in range(1, amount + 1)]
    largest = bound if full else min(bound, max(-(-total // amount), total * portions[0] // sum(portions)))
    least = 1 if total - largest >= amount - 1 else 0
    counts, rest = [largest] + [least] * (amount - 1), total - largest - least * (amount - 1)
    while rest > 0:
        candidates = [i for i in range(1, amount) if counts[i] < largest] or [i for i in range(1, amount) if counts[i] < bound]
        mass, left = sum([portions[i] for i in candidates]), rest
        for i in candidates:
            more = min(bound - counts[i], max(1, left * portions[i] // mass), rest)
            counts[i] = counts[i] + more
            rest = rest - more
    return np.array(counts)


def gaussian(key, extent, width, reach, cuts=(), kind=jnp.bfloat16):
    drawn = jax.random.normal(key, extent, jnp.float32) * width
    if len(cuts) > 0:
        drawn = block_levels(key, extent, cuts, -0.22, 0.18) * drawn
    return jnp.clip(drawn, min=-reach, max=reach).astype(kind)


def setup_inputs(seed: int = 0) -> dict:
    arg_keys = jax.random.split(jax.random.key(seed), 5)
    inverse = draw_inverse(jax.random.fold_in(arg_keys[4], 71), 0)
    tiles = gaussian(arg_keys[1], (TILES, 2 * BLOCK), 1.0, 6.0, ((0, 32),))
    tile_dest_keys = jax.random.split(jax.random.fold_in(arg_keys[2], 1), TILES // TPD)
    tile_dest_turns = jax.random.permutation(jax.random.fold_in(arg_keys[2], 3), TILES // TPD)
    tile_dest = jax.vmap(lambda own, number: assign_block(jax.random.fold_in(arg_keys[2], 2), own, number, TPD, N_LAYER * N_LAT, 1, CAP, 2))(tile_dest_keys, tile_dest_turns).reshape((TILES, 1))
    tile_code = touch_ends(jax.random.randint(arg_keys[3], (TILES,), 0, SRC * DEP * NB), jax.random.fold_in(arg_keys[3], 1), 0, (SRC * DEP * NB) - 1).astype(jnp.int32)
    return {"inverse": inverse, "tiles": tiles, "tile_dest": tile_dest, "tile_code": tile_code}


def apply_block(matrix, vectors):
    return jnp.einsum("bij,bsj->bsi", matrix, vectors, precision=lax.Precision.HIGHEST)


def reference(inverse, tiles, tile_dest, tile_code):
    trace_len = 2 * BLOCK
    far_rows = trace_len * (DEP - 1)
    target = tile_dest[:, 0]
    layer_at = target // N_LAT
    block_at = (target % N_LAT) * NB + tile_code % NB
    plane_at = (tile_code // NB) % DEP
    source_at = tile_code // (NB * DEP)
    segment = ((layer_at * BLOCKS + block_at) * SRC + source_at) * DEP + plane_at
    summed = jax.ops.segment_sum(tiles.astype(jnp.float32), segment.astype(jnp.int32), num_segments=N_LAYER * BLOCKS * SRC * DEP)
    source_field = lax.optimization_barrier(summed.reshape(N_LAYER, BLOCKS, SRC, M).astype(jnp.bfloat16))

    def solve_layer(pieces):
        matrix, vectors = pieces
        return apply_block(matrix.astype(jnp.float32), vectors.astype(jnp.float32))

    local_solve = lax.map(solve_layer, (inverse, source_field))
    down_matrix = inverse[:, :, far_rows:, :trace_len].astype(jnp.float32)
    up_matrix = inverse[:, :, :trace_len, far_rows:].astype(jnp.float32)
    empty = jnp.zeros((BLOCKS, SRC, trace_len), jnp.float32)

    def sweep_step(before, pieces):
        matrix, offset = pieces
        after = apply_block(matrix, before) + offset
        return after, before

    _, from_above = lax.scan(sweep_step, empty, (down_matrix, local_solve[:, :, :, far_rows:]))
    _, from_below = lax.scan(sweep_step, empty, (up_matrix, local_solve[:, :, :, :trace_len]), reverse=True)
    above_trace = lax.optimization_barrier(from_above.astype(jnp.bfloat16))
    below_trace = lax.optimization_barrier(from_below.astype(jnp.bfloat16))

    def finish_layer(pieces):
        matrix, local_part, above_part, below_part = pieces
        matrix_wide = matrix.astype(jnp.float32)
        result = local_part + apply_block(matrix_wide[:, :, :trace_len], above_part.astype(jnp.float32))
        return result + apply_block(matrix_wide[:, :, far_rows:], below_part.astype(jnp.float32))

    return lax.map(finish_layer, (inverse, local_solve, above_trace, below_trace))
```

```python
import functools

import jax
import jax.numpy as jnp
from jax import lax
from jax.experimental import pallas as pl
from jax.experimental.pallas import tpu as pltpu
from jax.sharding import PartitionSpec as P

MESH = pl.DeviceIdType.MESH
F32 = jnp.float32
BF16 = jnp.bfloat16
GROUP = 32


def nt(vectors, matrix):
    return lax.dot_general(vectors, matrix, (((1,), (1,)), ((), ())), preferred_element_type=F32)


def split(values):
    high = values.astype(BF16)
    return high, (values - high.astype(F32)).astype(BF16)


def apply_wide(values, matrix):
    high, low = split(values)
    both = nt(jnp.concatenate([high.astype(F32), low.astype(F32)], axis=0).astype(BF16), matrix)
    rows = values.shape[0]
    return both[:rows] + both[rows:]


def kernel(
    layers, lateral,
    inv, tiles, dest, code, out,
    send, recv, chalf, ohalf, far, comp_hi, comp_lo, acc, give, po, cin, oin, fout,
    load_sem, send_sem, recv_sem, far_send, far_recv, po_send, po_recv, c_send, c_recv, o_send, o_recv,
):
    layer = lax.axis_index("layer")
    lat = lax.axis_index("lat")
    devices = layers * lateral
    me = layer * lateral + lat
    x = lax.rem(layer, 2)
    group = layer // 2
    groups = layers // 2
    step = 2 * x - 1
    place = jnp.where(x == 1, group, groups - 1 - group)
    blocks, size, r = chalf.shape
    src = acc.shape[1]
    count = tiles.shape[0]
    mine = pl.multiple_of((1 - x) * r, r)
    other = pl.multiple_of(x * r, r)

    loads = [
        pltpu.make_async_copy(inv.at[0, :, :, pl.ds(mine, r)], chalf, load_sem.at[0]),
        pltpu.make_async_copy(inv.at[0, :, :, pl.ds(other, r)], ohalf, load_sem.at[1]),
    ]
    for load in loads:
        load.start()

    barrier = pltpu.get_barrier_semaphore()

    @pl.loop(1, devices)
    def _(i):
        to = lax.rem(me + i, devices)
        pl.semaphore_signal(
            barrier, inc=1, device_id=(to // lateral, lax.rem(to, lateral)), device_id_type=MESH
        )

    row_t = lax.broadcasted_iota(jnp.int32, (count, count), 0)
    col_t = lax.broadcasted_iota(jnp.int32, (count, count), 1)
    named = jnp.broadcast_to(dest[...], (count, count))
    target = jnp.sum(jnp.where(row_t == col_t, named, 0), axis=0, keepdims=True)
    order = jnp.sum(
        jnp.where((named == target) & (row_t < col_t), 1, 0), axis=0, keepdims=True
    )
    codes = jnp.broadcast_to(code[...], (count, count)) + 1
    code_col = jnp.sum(jnp.where(row_t == col_t, codes, 0), axis=1, keepdims=True)
    half = r // 2
    parts = [
        tiles[:, :half],
        tiles[:, half:],
        jnp.broadcast_to(code_col, (count, half)).astype(F32).astype(BF16),
    ]
    shape_w = (GROUP * 8, count)
    row_w = lax.broadcasted_iota(jnp.int32, shape_w, 0)
    q_w = row_w % 8
    slot_w = jnp.where(q_w < 4, q_w // 2, q_w - 4)
    kind_w = jnp.where(q_w < 4, q_w % 2, jnp.where(q_w < 6, 2, 3))

    def pack(chunk):
        hit = (target == chunk * GROUP + row_w // 8) & (order == slot_w)
        message = jnp.zeros((GROUP * 8, half), F32)
        for kind, part in enumerate(parts):
            picks = jnp.where(hit & (kind_w == kind), 1.0, 0.0).astype(BF16)
            message = message + jnp.dot(picks, part, preferred_element_type=F32)
        send[pl.ds(chunk * GROUP, GROUP)] = message.reshape(GROUP, 8, half).astype(BF16)

    if devices == GROUP:
        pack(0)
    else:
        pl.loop(0, devices // GROUP)(pack)
    recv[me] = send[me]

    pl.semaphore_wait(barrier, devices - 1)

    @pl.loop(1, devices)
    def _(i):
        to = lax.rem(me + i, devices)
        pltpu.make_async_remote_copy(
            src_ref=send.at[to],
            dst_ref=recv.at[me],
            send_sem=send_sem,
            recv_sem=recv_sem,
            device_id=(to // lateral, lax.rem(to, lateral)),
            device_id_type=MESH,
        ).start()

    partner = (layer - step, lat)
    far_copy = pltpu.make_async_remote_copy(
        src_ref=inv.at[0, :, pl.ds(mine, r), pl.ds(other, r)],
        dst_ref=far,
        send_sem=far_send,
        recv_sem=far_recv,
        device_id=partner,
        device_id_type=MESH,
    )
    far_copy.start()

    for load in loads:
        load.wait()
    far_copy.wait_recv()
    for b in range(blocks):
        product = jnp.dot(
            chalf[b, pl.ds(other, r), :], far[b], preferred_element_type=F32
        )
        high, low = split(product)
        comp_hi[b] = high
        comp_lo[b] = low

    rest = pl.ds(0, devices - 1)
    pltpu.make_async_copy(recv.at[rest], recv.at[rest], recv_sem).wait()

    shape_u = (GROUP, 8, half)
    q_u = lax.broadcasted_iota(jnp.int32, shape_u, 1)
    lane = lax.broadcasted_iota(jnp.int32, shape_u, 2)
    s_of, half_of, plane_of, block_of = lane % 8, (lane // 8) % 2, (lane // 16) % 2, lane // 32
    wanted = (((s_of * 2 + plane_of) * blocks + block_of) + 1).astype(F32)
    usable = (q_u < 4) & (q_u % 2 == half_of) & (lane < 64)

    def unpack(chunk):
        got = recv[pl.ds(chunk * GROUP, GROUP)].astype(F32)
        named_code = jnp.where(q_u < 2, got[:, 4:5, :], got[:, 5:6, :])
        table = jnp.where(usable & (named_code == wanted), 1.0, 0.0)
        return lax.dot_general(
            table.reshape(GROUP * 8, half).astype(BF16),
            got.reshape(GROUP * 8, half).astype(BF16),
            (((0,), (0,)), ((), ())),
            preferred_element_type=F32,
        )

    if devices == GROUP:
        field = unpack(0)
    else:
        field = lax.fori_loop(
            0, devices // GROUP, lambda i, total: total + unpack(i), jnp.zeros((half, half), F32)
        )

    owned = []
    upper = x == 1
    for b in range(blocks):
        rows = [field[32 * b + 8 * k : 32 * b + 8 * k + 8] for k in range(4)]
        top = jnp.concatenate(rows[:2], axis=1)
        bottom = jnp.concatenate(rows[2:], axis=1)
        own = jnp.where(upper, top, bottom).astype(BF16)
        away = jnp.where(upper, bottom, top).astype(BF16)
        local = nt(own, chalf[b]) + nt(away, ohalf[b])
        acc[b] = local
        give[b] = jnp.where(upper, local[:, :r], local[:, r:])
        owned.append(jnp.where(upper, local[:, r:], local[:, :r]))

    po_copy = pltpu.make_async_remote_copy(
        src_ref=give, dst_ref=po, send_sem=po_send, recv_sem=po_recv,
        device_id=partner, device_id_type=MESH,
    )
    po_copy.start()
    po_copy.wait_recv()
    for b in range(blocks):
        fout[b] = apply_wide(po[b], chalf[b, pl.ds(other, r), :]) + owned[b]

    onward = layer + 2 * step
    c_copy = pltpu.make_async_remote_copy(
        src_ref=fout, dst_ref=cin, send_sem=c_send, recv_sem=c_recv,
        device_id=(onward, lat), device_id_type=MESH,
    )
    o_copy = pltpu.make_async_remote_copy(
        src_ref=fout, dst_ref=oin, send_sem=o_send, recv_sem=o_recv,
        device_id=(onward - step, lat), device_id_type=MESH,
    )
    last = place == groups - 1
    first = place == 0

    def forward():
        @pl.when(jnp.logical_not(last))
        def _():
            c_copy.start()
            o_copy.start()

    def chain():
        @pl.when(first)
        def _():
            forward()
            for b in range(blocks):
                acc[b] = acc[b] + nt(po[b].astype(BF16), chalf[b])

        @pl.when(jnp.logical_not(first))
        def _():
            c_copy.wait_recv()

            @pl.when(jnp.logical_not(last))
            def _():
                for b in range(blocks):
                    state = cin[b]
                    fout[b] = (
                        fout[b]
                        + apply_wide(state, comp_hi[b])
                        + nt(state.astype(BF16), comp_lo[b])
                    )

            forward()
            for b in range(blocks):
                trace = apply_wide(cin[b], far[b]) + po[b]
                acc[b] = acc[b] + nt(trace.astype(BF16), chalf[b])

    def opposite():
        @pl.when(jnp.logical_not(last))
        def _():
            o_copy.wait_recv()
            for b in range(blocks):
                acc[b] = acc[b] + nt(oin[b].astype(BF16), ohalf[b])

    early = 2 * place < groups

    @pl.when(early)
    def _():
        chain()
        opposite()

    @pl.when(jnp.logical_not(early))
    def _():
        opposite()
        chain()

    for b in range(blocks):
        out[0, b] = acc[b]

    @pl.when(jnp.logical_not(last))
    def _():
        c_copy.wait_send()
        o_copy.wait_send()

    po_copy.wait_send()
    far_copy.wait_send()
    pltpu.make_async_copy(send.at[rest], send.at[rest], send_sem).wait()


def body(layers, lateral, inverse, tiles, tile_dest, tile_code):
    devices = layers * lateral
    _, blocks, size, _ = inverse.shape
    r = tiles.shape[1]
    src = 8
    dma = pltpu.SemaphoreType.DMA
    small = (blocks, src, r)
    vmem = pl.BlockSpec(memory_space=pltpu.VMEM)
    return pl.pallas_call(
        functools.partial(kernel, layers, lateral),
        out_shape=jax.ShapeDtypeStruct((1, blocks, src, size), F32),
        in_specs=[pl.BlockSpec(memory_space=pl.ANY), vmem, vmem, vmem],
        out_specs=vmem,
        scratch_shapes=[
            pltpu.VMEM((devices, 8, r // 2), BF16),
            pltpu.VMEM((devices, 8, r // 2), BF16),
            pltpu.VMEM((blocks, size, r), BF16),
            pltpu.VMEM((blocks, size, r), BF16),
            pltpu.VMEM((blocks, r, r), BF16),
            pltpu.VMEM((blocks, r, r), BF16),
            pltpu.VMEM((blocks, r, r), BF16),
            pltpu.VMEM((blocks, src, size), F32),
            pltpu.VMEM(small, F32),
            pltpu.VMEM(small, F32),
            pltpu.VMEM(small, F32),
            pltpu.VMEM(small, F32),
            pltpu.VMEM(small, F32),
            dma((2,)),
        ]
        + [dma] * 10,
        compiler_params=pltpu.CompilerParams(
            collective_id=0, has_side_effects=True, vmem_limit_bytes=48 * 1024 * 1024
        ),
        name="sweep",
    )(inverse, tiles, tile_dest, tile_code.reshape(1, -1))


def solution(mesh):
    in_specs = (
        P("layer", "lat", None, None),
        P(("layer", "lat"), None),
        P(("layer", "lat"), None),
        P(("layer", "lat")),
    )
    out_specs = P("layer", "lat", None, None)
    return jax.shard_map(
        functools.partial(body, mesh.shape["layer"], mesh.shape["lat"]),
        mesh=mesh, in_specs=in_specs, out_specs=out_specs, check_vma=False,
    )
```

```python
import functools

import jax
import jax.numpy as jnp
from jax import lax
from jax.experimental import pallas as pl
from jax.experimental.pallas import tpu as pltpu
from jax.sharding import PartitionSpec as P

MESH = pl.DeviceIdType.MESH
F32 = jnp.float32
BF16 = jnp.bfloat16
GROUP = 32


def nt(vectors, matrix):
    return lax.dot_general(vectors, matrix, (((1,), (1,)), ((), ())), preferred_element_type=F32)


def kernel(
    layers, lateral,
    inv, tiles_in, dest_in, code_in, out,
    tiles, dest, code, send, recv, chalf, ohalf, far, comp, acc, base, give, po, cin, oin, fout,
    small_sem, load_sem, send_sem, recv_sem, far_send, far_recv, po_send, po_recv, c_send, c_recv, o_send, o_recv,
):
    layer = lax.axis_index("layer")
    lat = lax.axis_index("lat")
    devices = layers * lateral
    me = layer * lateral + lat
    x = lax.rem(layer, 2)
    group = layer // 2
    groups = layers // 2
    step = 2 * x - 1
    place = jnp.where(x == 1, group, groups - 1 - group)
    blocks, size, r = chalf.shape
    src = acc.shape[1]
    count = tiles.shape[0]
    mine = pl.multiple_of((1 - x) * r, r)
    other = pl.multiple_of(x * r, r)

    smalls = [
        pltpu.make_async_copy(source, target, small_sem.at[i])
        for i, (source, target) in enumerate(((tiles_in, tiles), (dest_in, dest), (code_in, code)))
    ]
    for load in smalls:
        load.start()
    loads = [
        pltpu.make_async_copy(inv.at[0, :, :, pl.ds(mine, r)], chalf, load_sem.at[0]),
        pltpu.make_async_copy(inv.at[0, :, :, pl.ds(other, r)], ohalf, load_sem.at[1]),
    ]

    barrier = pltpu.get_barrier_semaphore()

    @pl.loop(1, devices)
    def _(i):
        to = lax.rem(me + i, devices)
        pl.semaphore_signal(
            barrier, inc=1, device_id=(to // lateral, lax.rem(to, lateral)), device_id_type=MESH
        )

    for load in loads:
        load.start()
    for load in smalls:
        load.wait()

    row_t = lax.broadcasted_iota(jnp.int32, (count, count), 0)
    col_t = lax.broadcasted_iota(jnp.int32, (count, count), 1)
    target = dest[...]
    across = jnp.broadcast_to(target, (count, count))
    named = jnp.sum(jnp.where(row_t == col_t, across, 0), axis=1, keepdims=True)
    order = jnp.sum(
        jnp.where((named == target) & (row_t < col_t), 1, 0), axis=0, keepdims=True
    )
    codes = jnp.broadcast_to(code[...], (count, count)) + 1
    code_col = jnp.sum(jnp.where(row_t == col_t, codes, 0), axis=1, keepdims=True)
    half = r // 2
    parts = [
        tiles[:, :half],
        tiles[:, half:],
        jnp.broadcast_to(code_col, (count, half)).astype(F32).astype(BF16),
    ]
    shape_w = (GROUP * 8, count)
    row_w = lax.broadcasted_iota(jnp.int32, shape_w, 0)
    q_w = row_w % 8
    slot_w = jnp.where(q_w < 4, q_w // 2, q_w - 4)
    kind_w = jnp.where(q_w < 4, q_w % 2, jnp.where(q_w < 6, 2, 3))

    def pack(chunk):
        hit = (target == chunk * GROUP + row_w // 8) & (order == slot_w)
        message = jnp.zeros((GROUP * 8, half), F32)
        for kind, part in enumerate(parts):
            picks = jnp.where(hit & (kind_w == kind), 1.0, 0.0).astype(BF16)
            message = message + jnp.dot(picks, part, preferred_element_type=F32)
        send[pl.ds(chunk * GROUP, GROUP)] = message.reshape(GROUP, 8, half).astype(BF16)

    if devices == GROUP:
        pack(0)
    else:
        pl.loop(0, devices // GROUP)(pack)
    recv[me] = send[me]

    pl.semaphore_wait(barrier, devices - 1)

    @pl.loop(1, devices)
    def _(i):
        to = lax.rem(me + i, devices)
        pltpu.make_async_remote_copy(
            src_ref=send.at[to],
            dst_ref=recv.at[me],
            send_sem=send_sem,
            recv_sem=recv_sem,
            device_id=(to // lateral, lax.rem(to, lateral)),
            device_id_type=MESH,
        ).start()

    partner = (layer - step, lat)
    far_copy = pltpu.make_async_remote_copy(
        src_ref=inv.at[0, :, pl.ds(mine, r), pl.ds(other, r)],
        dst_ref=far,
        send_sem=far_send,
        recv_sem=far_recv,
        device_id=partner,
        device_id_type=MESH,
    )
    far_copy.start()

    for load in loads:
        load.wait()

    rest = pl.ds(0, devices - 1)
    pltpu.make_async_copy(recv.at[rest], recv.at[rest], recv_sem).wait()

    shape_u = (GROUP, 8, half)
    q_u = lax.broadcasted_iota(jnp.int32, shape_u, 1)
    lane = lax.broadcasted_iota(jnp.int32, shape_u, 2)
    s_of, half_of, plane_of, block_of = lane % 8, (lane // 8) % 2, (lane // 16) % 2, lane // 32
    wanted = (((s_of * 2 + plane_of) * blocks + block_of) + 1).astype(F32)
    usable = (q_u < 4) & (q_u % 2 == half_of) & (lane < 64)

    def unpack(chunk):
        got = recv[pl.ds(chunk * GROUP, GROUP)].astype(F32)
        named_code = jnp.where(q_u < 2, got[:, 4:5, :], got[:, 5:6, :])
        table = jnp.where(usable & (named_code == wanted), 1.0, 0.0)
        return lax.dot_general(
            table.reshape(GROUP * 8, half).astype(BF16),
            got.reshape(GROUP * 8, half).astype(BF16),
            (((0,), (0,)), ((), ())),
            preferred_element_type=F32,
        )

    if devices == GROUP:
        field = unpack(0)
    else:
        field = lax.fori_loop(
            0, devices // GROUP, lambda i, total: total + unpack(i), jnp.zeros((half, half), F32)
        )

    owned = []
    upper = x == 1
    for b in range(blocks):
        rows = [field[32 * b + 8 * k : 32 * b + 8 * k + 8] for k in range(4)]
        top = jnp.concatenate(rows[:2], axis=1)
        bottom = jnp.concatenate(rows[2:], axis=1)
        own = jnp.where(upper, top, bottom).astype(BF16)
        away = jnp.where(upper, bottom, top).astype(BF16)
        local = nt(own, chalf[b]) + nt(away, ohalf[b])
        acc[b] = local
        give[b] = jnp.where(upper, local[:, :r], local[:, r:]).astype(BF16)
        owned.append(jnp.where(upper, local[:, r:], local[:, :r]))

    po_copy = pltpu.make_async_remote_copy(
        src_ref=give, dst_ref=po, send_sem=po_send, recv_sem=po_recv,
        device_id=partner, device_id_type=MESH,
    )
    po_copy.start()
    po_copy.wait_recv()
    for b in range(blocks):
        total = nt(po[b], chalf[b, pl.ds(other, r), :]) + owned[b]
        base[b] = total
        fout[b] = total.astype(BF16)

    onward = layer + 2 * step
    c_copy = pltpu.make_async_remote_copy(
        src_ref=fout, dst_ref=cin, send_sem=c_send, recv_sem=c_recv,
        device_id=(onward, lat), device_id_type=MESH,
    )
    o_copy = pltpu.make_async_remote_copy(
        src_ref=fout, dst_ref=oin, send_sem=o_send, recv_sem=o_recv,
        device_id=(onward - step, lat), device_id_type=MESH,
    )
    last = place == groups - 1
    first = place == 0

    def forward():
        @pl.when(jnp.logical_not(last))
        def _():
            c_copy.start()
            o_copy.start()

    @pl.when(first)
    def _():
        forward()

    far_copy.wait_recv()

    @pl.when(jnp.logical_not(first | last))
    def _():
        for b in range(blocks):
            comp[b] = jnp.dot(
                chalf[b, pl.ds(other, r), :], far[b], preferred_element_type=F32
            ).astype(BF16)

    def chain():
        @pl.when(first)
        def _():
            for b in range(blocks):
                acc[b] = acc[b] + nt(po[b], chalf[b])

        @pl.when(jnp.logical_not(first))
        def _():
            c_copy.wait_recv()

            @pl.when(jnp.logical_not(last))
            def _():
                for b in range(blocks):
                    fout[b] = (base[b] + nt(cin[b], comp[b])).astype(BF16)

            forward()
            for b in range(blocks):
                trace = nt(cin[b], far[b]) + po[b].astype(F32)
                acc[b] = acc[b] + nt(trace.astype(BF16), chalf[b])

    def opposite():
        @pl.when(jnp.logical_not(last))
        def _():
            o_copy.wait_recv()
            for b in range(blocks):
                acc[b] = acc[b] + nt(oin[b], ohalf[b])

    early = 2 * place < groups

    @pl.when(early)
    def _():
        chain()
        opposite()

    @pl.when(jnp.logical_not(early))
    def _():
        opposite()
        chain()

    for b in range(blocks):
        out[0, b] = acc[b]

    @pl.when(jnp.logical_not(last))
    def _():
        c_copy.wait_send()
        o_copy.wait_send()

    po_copy.wait_send()
    far_copy.wait_send()
    pltpu.make_async_copy(send.at[rest], send.at[rest], send_sem).wait()


def body(layers, lateral, inverse, tiles, tile_dest, tile_code):
    devices = layers * lateral
    _, blocks, size, _ = inverse.shape
    r = tiles.shape[1]
    src = 8
    dma = pltpu.SemaphoreType.DMA
    small = (blocks, src, r)
    vmem = pl.BlockSpec(memory_space=pltpu.VMEM)
    return pl.pallas_call(
        functools.partial(kernel, layers, lateral),
        out_shape=jax.ShapeDtypeStruct((1, blocks, src, size), F32),
        in_specs=[pl.BlockSpec(memory_space=pltpu.HBM)] * 4,
        out_specs=vmem,
        scratch_shapes=[
            pltpu.VMEM(tiles.shape, BF16),
            pltpu.VMEM((1, tiles.shape[0]), jnp.int32),
            pltpu.VMEM((1, tiles.shape[0]), jnp.int32),
            pltpu.VMEM((devices, 8, r // 2), BF16),
            pltpu.VMEM((devices, 8, r // 2), BF16),
            pltpu.VMEM((blocks, size, r), BF16),
            pltpu.VMEM((blocks, size, r), BF16),
            pltpu.VMEM((blocks, r, r), BF16),
            pltpu.VMEM((blocks, r, r), BF16),
            pltpu.VMEM((blocks, src, size), F32),
            pltpu.VMEM(small, F32),
            pltpu.VMEM(small, BF16),
            pltpu.VMEM(small, BF16),
            pltpu.VMEM(small, BF16),
            pltpu.VMEM(small, BF16),
            pltpu.VMEM(small, BF16),
            dma((3,)),
            dma((2,)),
        ]
        + [dma] * 10,
        compiler_params=pltpu.CompilerParams(
            collective_id=0, has_side_effects=True, vmem_limit_bytes=48 * 1024 * 1024
        ),
        name="sweep",
    )(
        *(
            pltpu.with_memory_space_constraint(array, pltpu.HBM)
            for array in (inverse, tiles, tile_dest.reshape(1, -1), tile_code.reshape(1, -1))
        )
    )


def solution(mesh):
    in_specs = (
        P("layer", "lat", None, None),
        P(("layer", "lat"), None),
        P(("layer", "lat"), None),
        P(("layer", "lat")),
    )
    out_specs = P("layer", "lat", None, None)
    return jax.shard_map(
        functools.partial(body, mesh.shape["layer"], mesh.shape["lat"]),
        mesh=mesh, in_specs=in_specs, out_specs=out_specs, check_vma=False,
    )
```

```python
import functools

import jax
import jax.numpy as jnp
from jax import lax
from jax.experimental import pallas as pl
from jax.experimental.pallas import tpu as pltpu
from jax.sharding import PartitionSpec as P

MESH = pl.DeviceIdType.MESH
F32 = jnp.float32
BF16 = jnp.bfloat16
GROUP = 32


def nt(vectors, matrix):
    return lax.dot_general(vectors, matrix, (((1,), (1,)), ((), ())), preferred_element_type=F32)


def kernel(
    layers, lateral,
    inv, tiles_in, dest_in, code_in, out,
    tiles, dest, code, send, recv, chalf, ohalf, far, comp, acc, base, give, po, cin, oin, fout,
    small_sem, load_sem, send_sem, recv_sem, far_send, far_recv, po_send, po_recv, c_send, c_recv, o_send, o_recv,
):
    layer = lax.axis_index("layer")
    lat = lax.axis_index("lat")
    devices = layers * lateral
    me = layer * lateral + lat
    x = lax.rem(layer, 2)
    group = layer // 2
    groups = layers // 2
    step = 2 * x - 1
    place = jnp.where(x == 1, group, groups - 1 - group)
    blocks, size, r = chalf.shape
    src = acc.shape[1]
    count = tiles.shape[0]
    mine = pl.multiple_of((1 - x) * r, r)
    other = pl.multiple_of(x * r, r)

    barrier = pltpu.get_barrier_semaphore()

    def wrap(index, length):
        return jnp.where(index >= length, index - length, index)

    def others(visit):
        def visit_layer(i):
            to = jnp.where(layer < layers // 2, layers - 1 - i, i)

            def visit_lat(across):
                visit(to, wrap(lat + across, lateral))

            for across in range(1, lateral):
                visit_lat(across)

            @pl.when(to != layer)
            def _():
                visit_lat(0)

        if devices == GROUP:
            for i in range(layers):
                visit_layer(i)
        else:
            pl.loop(0, layers)(visit_layer)

    def greet(to_layer, to_lat):
        pl.semaphore_signal(
            barrier, inc=1, device_id=(to_layer, to_lat), device_id_type=MESH
        )

    others(greet)

    smalls = [
        pltpu.make_async_copy(source, target, small_sem.at[i])
        for i, (source, target) in enumerate(((tiles_in, tiles), (dest_in, dest), (code_in, code)))
    ]
    for load in smalls:
        load.start()
    loads = [
        pltpu.make_async_copy(inv.at[0, :, :, pl.ds(mine, r)], chalf, load_sem.at[0]),
        pltpu.make_async_copy(inv.at[0, :, :, pl.ds(other, r)], ohalf, load_sem.at[1]),
    ]

    for load in loads:
        load.start()
    for load in smalls:
        load.wait()

    row_t = lax.broadcasted_iota(jnp.int32, (count, count), 0)
    col_t = lax.broadcasted_iota(jnp.int32, (count, count), 1)
    target = dest[...]
    across = jnp.broadcast_to(target, (count, count))
    named = jnp.sum(jnp.where(row_t == col_t, across, 0), axis=1, keepdims=True)
    order = jnp.sum(
        jnp.where((named == target) & (row_t < col_t), 1, 0), axis=0, keepdims=True
    )
    codes = jnp.broadcast_to(code[...], (count, count)) + 1
    code_col = jnp.sum(jnp.where(row_t == col_t, codes, 0), axis=1, keepdims=True)
    half = r // 2
    parts = [
        tiles[:, :half],
        tiles[:, half:],
        jnp.broadcast_to(code_col, (count, half)).astype(F32).astype(BF16),
    ]
    shape_w = (GROUP * 8, count)
    row_w = lax.broadcasted_iota(jnp.int32, shape_w, 0)
    q_w = row_w % 8
    slot_w = jnp.where(q_w < 4, q_w // 2, q_w - 4)
    kind_w = jnp.where(q_w < 4, q_w % 2, jnp.where(q_w < 6, 2, 3))

    def pack(chunk):
        hit = (target == chunk * GROUP + row_w // 8) & (order == slot_w)
        message = jnp.zeros((GROUP * 8, half), F32)
        for kind, part in enumerate(parts):
            picks = jnp.where(hit & (kind_w == kind), 1.0, 0.0).astype(BF16)
            message = message + jnp.dot(picks, part, preferred_element_type=F32)
        send[pl.ds(chunk * GROUP, GROUP)] = message.reshape(GROUP, 8, half).astype(BF16)

    if devices == GROUP:
        pack(0)
    else:
        pl.loop(0, devices // GROUP)(pack)
    recv[me] = send[me]

    pl.semaphore_wait(barrier, devices - 1)

    def route(to_layer, to_lat):
        pltpu.make_async_remote_copy(
            src_ref=send.at[to_layer * lateral + to_lat],
            dst_ref=recv.at[me],
            send_sem=send_sem,
            recv_sem=recv_sem,
            device_id=(to_layer, to_lat),
            device_id_type=MESH,
        ).start()

    others(route)

    partner = (layer - step, lat)
    far_copy = pltpu.make_async_remote_copy(
        src_ref=inv.at[0, :, pl.ds(mine, r), pl.ds(other, r)],
        dst_ref=far,
        send_sem=far_send,
        recv_sem=far_recv,
        device_id=partner,
        device_id_type=MESH,
    )
    far_copy.start()

    for load in loads:
        load.wait()

    rest = pl.ds(0, devices - 1)
    pltpu.make_async_copy(recv.at[rest], recv.at[rest], recv_sem).wait()

    shape_u = (GROUP, 8, half)
    q_u = lax.broadcasted_iota(jnp.int32, shape_u, 1)
    lane = lax.broadcasted_iota(jnp.int32, shape_u, 2)
    s_of, half_of, plane_of, block_of = lane % 8, (lane // 8) % 2, (lane // 16) % 2, lane // 32
    wanted = (((s_of * 2 + plane_of) * blocks + block_of) + 1).astype(F32)
    usable = (q_u < 4) & (q_u % 2 == half_of) & (lane < 64)

    def unpack(chunk):
        got = recv[pl.ds(chunk * GROUP, GROUP)].astype(F32)
        named_code = jnp.where(q_u < 2, got[:, 4:5, :], got[:, 5:6, :])
        table = jnp.where(usable & (named_code == wanted), 1.0, 0.0)
        return lax.dot_general(
            table.reshape(GROUP * 8, half).astype(BF16),
            got.reshape(GROUP * 8, half).astype(BF16),
            (((0,), (0,)), ((), ())),
            preferred_element_type=F32,
        )

    if devices == GROUP:
        field = unpack(0)
    else:
        field = lax.fori_loop(
            0, devices // GROUP, lambda i, total: total + unpack(i), jnp.zeros((half, half), F32)
        )

    owned = []
    upper = x == 1
    for b in range(blocks):
        rows = [field[32 * b + 8 * k : 32 * b + 8 * k + 8] for k in range(4)]
        top = jnp.concatenate(rows[:2], axis=1)
        bottom = jnp.concatenate(rows[2:], axis=1)
        own = jnp.where(upper, top, bottom).astype(BF16)
        away = jnp.where(upper, bottom, top).astype(BF16)
        local = nt(own, chalf[b]) + nt(away, ohalf[b])
        acc[b] = local
        give[b] = jnp.where(upper, local[:, :r], local[:, r:]).astype(BF16)
        owned.append(jnp.where(upper, local[:, r:], local[:, :r]))

    po_copy = pltpu.make_async_remote_copy(
        src_ref=give, dst_ref=po, send_sem=po_send, recv_sem=po_recv,
        device_id=partner, device_id_type=MESH,
    )
    po_copy.start()
    po_copy.wait_recv()
    for b in range(blocks):
        total = nt(po[b], chalf[b, pl.ds(other, r), :]) + owned[b]
        base[b] = total
        fout[b] = total.astype(BF16)

    onward = layer + 2 * step
    c_copy = pltpu.make_async_remote_copy(
        src_ref=fout, dst_ref=cin, send_sem=c_send, recv_sem=c_recv,
        device_id=(onward, lat), device_id_type=MESH,
    )
    o_copy = pltpu.make_async_remote_copy(
        src_ref=fout, dst_ref=oin, send_sem=o_send, recv_sem=o_recv,
        device_id=(onward - step, lat), device_id_type=MESH,
    )
    last = place == groups - 1
    first = place == 0

    def forward():
        @pl.when(jnp.logical_not(last))
        def _():
            c_copy.start()
            o_copy.start()

    @pl.when(first)
    def _():
        forward()

    far_copy.wait_recv()

    @pl.when(jnp.logical_not(first | last))
    def _():
        for b in range(blocks):
            comp[b] = jnp.dot(
                chalf[b, pl.ds(other, r), :], far[b], preferred_element_type=F32
            ).astype(BF16)

    def chain():
        @pl.when(first)
        def _():
            for b in range(blocks):
                acc[b] = acc[b] + nt(po[b], chalf[b])

        @pl.when(jnp.logical_not(first))
        def _():
            c_copy.wait_recv()

            @pl.when(jnp.logical_not(last))
            def _():
                for b in range(blocks):
                    fout[b] = (base[b] + nt(cin[b], comp[b])).astype(BF16)

            forward()
            for b in range(blocks):
                trace = nt(cin[b], far[b]) + po[b].astype(F32)
                acc[b] = acc[b] + nt(trace.astype(BF16), chalf[b])

    def opposite():
        @pl.when(jnp.logical_not(last))
        def _():
            o_copy.wait_recv()
            for b in range(blocks):
                acc[b] = acc[b] + nt(oin[b], ohalf[b])

    early = 2 * place < groups

    @pl.when(early)
    def _():
        chain()
        opposite()

    @pl.when(jnp.logical_not(early))
    def _():
        opposite()
        chain()

    for b in range(blocks):
        out[0, b] = acc[b]

    @pl.when(jnp.logical_not(last))
    def _():
        c_copy.wait_send()
        o_copy.wait_send()

    po_copy.wait_send()
    far_copy.wait_send()
    pltpu.make_async_copy(send.at[rest], send.at[rest], send_sem).wait()


def body(layers, lateral, inverse, tiles, tile_dest, tile_code):
    devices = layers * lateral
    _, blocks, size, _ = inverse.shape
    r = tiles.shape[1]
    src = 8
    dma = pltpu.SemaphoreType.DMA
    small = (blocks, src, r)
    vmem = pl.BlockSpec(memory_space=pltpu.VMEM)
    return pl.pallas_call(
        functools.partial(kernel, layers, lateral),
        out_shape=jax.ShapeDtypeStruct((1, blocks, src, size), F32),
        in_specs=[pl.BlockSpec(memory_space=pltpu.HBM)] * 4,
        out_specs=vmem,
        scratch_shapes=[
            pltpu.VMEM(tiles.shape, BF16),
            pltpu.VMEM((1, tiles.shape[0]), jnp.int32),
            pltpu.VMEM((1, tiles.shape[0]), jnp.int32),
            pltpu.VMEM((devices, 8, r // 2), BF16),
            pltpu.VMEM((devices, 8, r // 2), BF16),
            pltpu.VMEM((blocks, size, r), BF16),
            pltpu.VMEM((blocks, size, r), BF16),
            pltpu.VMEM((blocks, r, r), BF16),
            pltpu.VMEM((blocks, r, r), BF16),
            pltpu.VMEM((blocks, src, size), F32),
            pltpu.VMEM(small, F32),
            pltpu.VMEM(small, BF16),
            pltpu.VMEM(small, BF16),
            pltpu.VMEM(small, BF16),
            pltpu.VMEM(small, BF16),
            pltpu.VMEM(small, BF16),
            dma((3,)),
            dma((2,)),
        ]
        + [dma] * 10,
        compiler_params=pltpu.CompilerParams(
            collective_id=0, has_side_effects=True, vmem_limit_bytes=48 * 1024 * 1024
        ),
        name="sweep",
    )(
        *(
            pltpu.with_memory_space_constraint(array, pltpu.HBM)
            for array in (inverse, tiles, tile_dest.reshape(1, -1), tile_code.reshape(1, -1))
        )
    )


def solution(mesh):
    in_specs = (
        P("layer", "lat", None, None),
        P(("layer", "lat"), None),
        P(("layer", "lat"), None),
        P(("layer", "lat")),
    )
    out_specs = P("layer", "lat", None, None)
    return jax.shard_map(
        functools.partial(body, mesh.shape["layer"], mesh.shape["lat"]),
        mesh=mesh, in_specs=in_specs, out_specs=out_specs, check_vma=False,
    )
```

```python
import functools

import jax
import jax.numpy as jnp
from jax import lax
from jax.experimental import pallas as pl
from jax.experimental.pallas import tpu as pltpu
from jax.sharding import PartitionSpec as P

MESH = pl.DeviceIdType.MESH
F32 = jnp.float32
BF16 = jnp.bfloat16
GROUP = 32


def nt(vectors, matrix):
    return lax.dot_general(vectors, matrix, (((1,), (1,)), ((), ())), preferred_element_type=F32)


def kernel(
    layers, lateral,
    inv, tiles_in, dest_in, code_in, out,
    tiles, dest, code, send, recv, chalf, ohalf, far, comp, acc, base, give, po, cin, oin, fout,
    small_sem, load_sem, send_sem, recv_sem, far_send, far_recv, po_send, po_recv, c_send, c_recv, o_send, o_recv,
):
    layer = lax.axis_index("layer")
    lat = lax.axis_index("lat")
    devices = layers * lateral
    me = layer * lateral + lat
    x = lax.rem(layer, 2)
    group = layer // 2
    groups = layers // 2
    step = 2 * x - 1
    place = jnp.where(x == 1, group, groups - 1 - group)
    blocks, size, r = chalf.shape
    src = acc.shape[1]
    count = tiles.shape[0]
    mine = pl.multiple_of((1 - x) * r, r)
    other = pl.multiple_of(x * r, r)

    barrier = pltpu.get_barrier_semaphore()

    def wrap(index, length):
        return jnp.where(index >= length, index - length, index)

    def others(visit):
        def visit_layer(i):
            to = jnp.where(layer < layers // 2, layers - 1 - i, i)

            def visit_lat(across):
                visit(to, wrap(lat + across, lateral))

            for across in range(1, lateral):
                visit_lat(across)

            @pl.when(to != layer)
            def _():
                visit_lat(0)

        if devices == GROUP:
            for i in range(layers):
                visit_layer(i)
        else:
            pl.loop(0, layers)(visit_layer)

    def greet(to_layer, to_lat):
        pl.semaphore_signal(
            barrier, inc=1, device_id=(to_layer, to_lat), device_id_type=MESH
        )

    others(greet)

    smalls = [
        pltpu.make_async_copy(source, target, small_sem.at[i])
        for i, (source, target) in enumerate(((tiles_in, tiles), (dest_in, dest), (code_in, code)))
    ]
    for load in smalls:
        load.start()
    loads = [
        pltpu.make_async_copy(inv.at[0, :, :, pl.ds(mine, r)], chalf, load_sem.at[0]),
        pltpu.make_async_copy(inv.at[0, :, :, pl.ds(other, r)], ohalf, load_sem.at[1]),
    ]

    for load in loads:
        load.start()
    for load in smalls:
        load.wait()

    row_t = lax.broadcasted_iota(jnp.int32, (count, count), 0)
    col_t = lax.broadcasted_iota(jnp.int32, (count, count), 1)
    target = dest[...]
    across = jnp.broadcast_to(target, (count, count))
    named = jnp.sum(jnp.where(row_t == col_t, across, 0), axis=1, keepdims=True)
    order = jnp.sum(
        jnp.where((named == target) & (row_t < col_t), 1, 0), axis=0, keepdims=True
    )
    codes = jnp.broadcast_to(code[...], (count, count)) + 1
    code_col = jnp.sum(jnp.where(row_t == col_t, codes, 0), axis=1, keepdims=True)
    half = r // 2
    parts = [
        tiles[:, :half],
        tiles[:, half:],
        jnp.broadcast_to(code_col, (count, half)).astype(F32).astype(BF16),
    ]
    shape_w = (GROUP * 8, count)
    row_w = lax.broadcasted_iota(jnp.int32, shape_w, 0)
    q_w = row_w % 8
    slot_w = jnp.where(q_w < 4, q_w // 2, q_w - 4)
    kind_w = jnp.where(q_w < 4, q_w % 2, jnp.where(q_w < 6, 2, 3))

    def pack(chunk):
        hit = (target == chunk * GROUP + row_w // 8) & (order == slot_w)
        message = jnp.zeros((GROUP * 8, half), F32)
        for kind, part in enumerate(parts):
            picks = jnp.where(hit & (kind_w == kind), 1.0, 0.0).astype(BF16)
            message = message + jnp.dot(picks, part, preferred_element_type=F32)
        send[pl.ds(chunk * GROUP, GROUP)] = message.reshape(GROUP, 8, half).astype(BF16)

    if devices == GROUP:
        pack(0)
    else:
        pl.loop(0, devices // GROUP)(pack)
    recv[me] = send[me]

    pl.semaphore_wait(barrier, devices - 1)

    partner = (layer - step, lat)
    far_copy = pltpu.make_async_remote_copy(
        src_ref=inv.at[0, :, pl.ds(mine, r), pl.ds(other, r)],
        dst_ref=far,
        send_sem=far_send,
        recv_sem=far_recv,
        device_id=partner,
        device_id_type=MESH,
    )
    far_copy.start()

    def route(to_layer, to_lat):
        pltpu.make_async_remote_copy(
            src_ref=send.at[to_layer * lateral + to_lat],
            dst_ref=recv.at[me],
            send_sem=send_sem,
            recv_sem=recv_sem,
            device_id=(to_layer, to_lat),
            device_id_type=MESH,
        ).start()

    others(route)

    for load in loads:
        load.wait()

    rest = pl.ds(0, devices - 1)
    pltpu.make_async_copy(recv.at[rest], recv.at[rest], recv_sem).wait()

    shape_u = (GROUP, 8, half)
    q_u = lax.broadcasted_iota(jnp.int32, shape_u, 1)
    lane = lax.broadcasted_iota(jnp.int32, shape_u, 2)
    s_of, half_of, plane_of, block_of = lane % 8, (lane // 8) % 2, (lane // 16) % 2, lane // 32
    wanted = (((s_of * 2 + plane_of) * blocks + block_of) + 1).astype(F32)
    usable = (q_u < 4) & (q_u % 2 == half_of) & (lane < 64)

    def unpack(chunk):
        got = recv[pl.ds(chunk * GROUP, GROUP)].astype(F32)
        named_code = jnp.where(q_u < 2, got[:, 4:5, :], got[:, 5:6, :])
        table = jnp.where(usable & (named_code == wanted), 1.0, 0.0)
        return lax.dot_general(
            table.reshape(GROUP * 8, half).astype(BF16),
            got.reshape(GROUP * 8, half).astype(BF16),
            (((0,), (0,)), ((), ())),
            preferred_element_type=F32,
        )

    if devices == GROUP:
        field = unpack(0)
    else:
        field = lax.fori_loop(
            0, devices // GROUP, lambda i, total: total + unpack(i), jnp.zeros((half, half), F32)
        )

    owned = []
    upper = x == 1
    for b in range(blocks):
        rows = [field[32 * b + 8 * k : 32 * b + 8 * k + 8] for k in range(4)]
        top = jnp.concatenate(rows[:2], axis=1)
        bottom = jnp.concatenate(rows[2:], axis=1)
        own = jnp.where(upper, top, bottom).astype(BF16)
        away = jnp.where(upper, bottom, top).astype(BF16)
        local = nt(own, chalf[b]) + nt(away, ohalf[b])
        acc[b] = local
        give[b] = jnp.where(upper, local[:, :r], local[:, r:]).astype(BF16)
        owned.append(jnp.where(upper, local[:, r:], local[:, :r]))

    po_copy = pltpu.make_async_remote_copy(
        src_ref=give, dst_ref=po, send_sem=po_send, recv_sem=po_recv,
        device_id=partner, device_id_type=MESH,
    )
    po_copy.start()
    po_copy.wait_recv()
    for b in range(blocks):
        total = nt(po[b], chalf[b, pl.ds(other, r), :]) + owned[b]
        base[b] = total
        fout[b] = total.astype(BF16)

    onward = layer + 2 * step
    c_copy = pltpu.make_async_remote_copy(
        src_ref=fout, dst_ref=cin, send_sem=c_send, recv_sem=c_recv,
        device_id=(onward, lat), device_id_type=MESH,
    )
    o_copy = pltpu.make_async_remote_copy(
        src_ref=fout, dst_ref=oin, send_sem=o_send, recv_sem=o_recv,
        device_id=(onward - step, lat), device_id_type=MESH,
    )
    last = place == groups - 1
    first = place == 0

    def forward():
        @pl.when(jnp.logical_not(last))
        def _():
            c_copy.start()
            o_copy.start()

    @pl.when(first)
    def _():
        forward()

    far_copy.wait_recv()

    @pl.when(jnp.logical_not(first | last))
    def _():
        for b in range(blocks):
            comp[b] = jnp.dot(
                chalf[b, pl.ds(other, r), :], far[b], preferred_element_type=F32
            ).astype(BF16)

    def chain():
        @pl.when(first)
        def _():
            for b in range(blocks):
                acc[b] = acc[b] + nt(po[b], chalf[b])

        @pl.when(jnp.logical_not(first))
        def _():
            c_copy.wait_recv()

            @pl.when(jnp.logical_not(last))
            def _():
                for b in range(blocks):
                    fout[b] = (base[b] + nt(cin[b], comp[b])).astype(BF16)

            forward()
            for b in range(blocks):
                trace = nt(cin[b], far[b]) + po[b].astype(F32)
                acc[b] = acc[b] + nt(trace.astype(BF16), chalf[b])

    def opposite():
        @pl.when(jnp.logical_not(last))
        def _():
            o_copy.wait_recv()
            for b in range(blocks):
                acc[b] = acc[b] + nt(oin[b], ohalf[b])

    early = 2 * place < groups

    @pl.when(early)
    def _():
        chain()
        opposite()

    @pl.when(jnp.logical_not(early))
    def _():
        opposite()
        chain()

    for b in range(blocks):
        out[0, b] = acc[b]

    @pl.when(jnp.logical_not(last))
    def _():
        c_copy.wait_send()
        o_copy.wait_send()

    po_copy.wait_send()
    far_copy.wait_send()
    pltpu.make_async_copy(send.at[rest], send.at[rest], send_sem).wait()


def body(layers, lateral, inverse, tiles, tile_dest, tile_code):
    devices = layers * lateral
    _, blocks, size, _ = inverse.shape
    r = tiles.shape[1]
    src = 8
    dma = pltpu.SemaphoreType.DMA
    small = (blocks, src, r)
    vmem = pl.BlockSpec(memory_space=pltpu.VMEM)
    return pl.pallas_call(
        functools.partial(kernel, layers, lateral),
        out_shape=jax.ShapeDtypeStruct((1, blocks, src, size), F32),
        in_specs=[pl.BlockSpec(memory_space=pltpu.HBM)] * 4,
        out_specs=vmem,
        scratch_shapes=[
            pltpu.VMEM(tiles.shape, BF16),
            pltpu.VMEM((1, tiles.shape[0]), jnp.int32),
            pltpu.VMEM((1, tiles.shape[0]), jnp.int32),
            pltpu.VMEM((devices, 8, r // 2), BF16),
            pltpu.VMEM((devices, 8, r // 2), BF16),
            pltpu.VMEM((blocks, size, r), BF16),
            pltpu.VMEM((blocks, size, r), BF16),
            pltpu.VMEM((blocks, r, r), BF16),
            pltpu.VMEM((blocks, r, r), BF16),
            pltpu.VMEM((blocks, src, size), F32),
            pltpu.VMEM(small, F32),
            pltpu.VMEM(small, BF16),
            pltpu.VMEM(small, BF16),
            pltpu.VMEM(small, BF16),
            pltpu.VMEM(small, BF16),
            pltpu.VMEM(small, BF16),
            dma((3,)),
            dma((2,)),
        ]
        + [dma] * 10,
        compiler_params=pltpu.CompilerParams(
            collective_id=0, has_side_effects=True, vmem_limit_bytes=48 * 1024 * 1024
        ),
        name="sweep",
    )(
        *(
            pltpu.with_memory_space_constraint(array, pltpu.HBM)
            for array in (inverse, tiles, tile_dest.reshape(1, -1), tile_code.reshape(1, -1))
        )
    )


def solution(mesh):
    in_specs = (
        P("layer", "lat", None, None),
        P(("layer", "lat"), None),
        P(("layer", "lat"), None),
        P(("layer", "lat")),
    )
    out_specs = P("layer", "lat", None, None)
    return jax.shard_map(
        functools.partial(body, mesh.shape["layer"], mesh.shape["lat"]),
        mesh=mesh, in_specs=in_specs, out_specs=out_specs, check_vma=False,
    )
```
